32 devices in a mesh: member: 8 (over z, x), cell: 4 (over y, core).
Axes of the slice: x: 2, y: 2, z: 4, core: 2. Of those that a mesh axis runs over, the one named last changes fastest.
Arguments:
- latent: bfloat16 [8, 6144, 1024], P('member', 'cell'), may hold values from -6 to 6
- w_in: bfloat16 [1024, 1024], replicated, may hold values from -0.1875 to 0.1875
- w_out: bfloat16 [1024, 96], replicated, may hold values from -0.1875 to 0.1875
- target: bfloat16 [96, 6144], P(None, 'cell'), may hold values from -6 to 6
- cell_mask: int32 [6144], P('cell'), may hold values 0 or 1
Outputs:
- grad_w_in: float32 [1024, 1024], P(('member', 'cell'))
- grad_w_out: float32 [1024, 96], P(('member', 'cell'))
The draws below stay inside these ranges and needn't reach their ends.
All inputs are finite; a program needn't handle non-finite values. No bound on the sum of `cell_mask` on one device may be relied on, other than what follows from the above.
Results may differ from the reference program's by a relative error of at most 0.0055.
Values may be sent and summed in bfloat16 or wider, within the bound.
A program may use at most 64 MiB of HBM per device.

```python
import jax
import jax.numpy as jnp
from jax import lax

LATENT = 1024
HIDDEN_SIZE = 1024
FIELDS = 96
CELLS = 6144
MEMBERS = 8


def plant(values, stream_key, low, top_value):
    longest = values.shape.index(max(values.shape))
    spots = []
    for shift in (0, 1):
        where = [jax.random.randint(jax.random.fold_in(stream_key, axis), (), 0, length) for axis, length in enumerate(values.shape)]
        where[longest] = (where[longest] + shift) % values.shape[longest]
        spots.append(tuple(where))
    return values.at[spots[0]].set(low).at[spots[1]].set(top_value)


def with_spikes(array, key, source, target, parts, factor):
    owner, partner = [(jnp.arange(array.shape[axis_at]) // (array.shape[axis_at] // parts)).reshape([-1 if axis == axis_at else 1 for axis in range(array.ndim)]) for axis_at in (source, target)]
    chosen = jax.random.permutation(key, parts)[partner]
    strong = (owner == chosen) | (owner == (partner + parts // 2) % parts)
    return jnp.where(strong, factor * array, array)


def levels(key, shape, shards, least, largest):
    def one(dim, shards_of):
        steps = jax.random.uniform(jax.random.fold_in(jax.random.fold_in(key, 6), dim), (shards_of,), jnp.float32, least / len(shards), largest / len(shards))
        return jnp.repeat(jnp.exp(steps), shape[dim] // shards_of).reshape((-1,) + (1,) * (len(shape) - dim - 1))

    factor_of = one(*shards[0])
    for cut in shards[1:]:
        factor_of = factor_of * one(*cut)
    return factor_of


def centred(key, extent, spread, reach, pieces=(), held_as=jnp.bfloat16):
    level = levels(key, extent, pieces, -0.22, 0.18) if pieces else 1.0
    result = jax.random.normal(key, extent, jnp.float32) * spread * level
    return jnp.minimum(jnp.maximum(result, -reach), reach).astype(held_as)


def heavy_noise(own_key, shape, deviation, most, cuts, heavy, dtype=jnp.bfloat16):
    values = deviation * jax.random.normal(own_key, shape, jnp.float32)
    if cuts:
        values = values * levels(own_key, shape, cuts, -0.22, 0.18)
    return jnp.clip(with_spikes(values, jax.random.fold_in(own_key, 3), *heavy), -most, most).astype(dtype)


def setup_inputs(seed: int = 0) -> dict:
    key_of = jax.random.split(jax.random.key(seed), 6)
    latent = heavy_noise(key_of[0], (MEMBERS, CELLS, LATENT), 1.0, 6.0, ((0, 8), (1, 4)), (1, 2, 4, 2.0))
    w_in = centred(key_of[1], (LATENT, HIDDEN_SIZE), LATENT ** -0.5, 0.1875)
    w_out = centred(key_of[2], (HIDDEN_SIZE, FIELDS), HIDDEN_SIZE ** -0.5, 0.1875)
    target = centred(key_of[3], (FIELDS, CELLS), 1.0, 6.0, ((1, 4),))
    cell_mask = plant((jax.random.randint(key_of[4], (CELLS,), 0, 4) < 3).astype(jnp.int32), jax.random.fold_in(key_of[4], 1), 0, 1)
    return dict(latent=latent, w_in=w_in, w_out=w_out, target=target, cell_mask=cell_mask)


def kernel_fn(diff):
    return diff / jnp.sqrt(1.0 + diff * diff)

def silu_slope(pre):
    gate = jax.nn.sigmoid(pre)
    return gate * (1.0 + pre * (1.0 - gate))

def decode(member_latent, w_in, w_out):
    pre = jnp.dot(member_latent, w_in, preferred_element_type=jnp.float32)
    hidden = jax.nn.silu(pre).astype(jnp.bfloat16)
    fields = lax.dot_general(w_out, hidden, (((0,), (1,)), ((), ())), preferred_element_type=jnp.float32).astype(jnp.bfloat16)
    return (pre, hidden, fields)

def reference(latent, w_in, w_out, target, cell_mask):
    members = latent.shape[0]
    cells = latent.shape[1]
    scale = 1.0 / jnp.sqrt(jnp.float32(cells))
    fields = lax.map(lambda one: decode(one, w_in, w_out)[2], latent)
    wide = fields.astype(jnp.float32)
    pair = lax.map(lambda own: lax.optimization_barrier(jnp.sum(kernel_fn(own[None] - wide), axis=0)), wide)
    weight = cell_mask.astype(jnp.float32) * scale / members
    own_term = kernel_fn(wide - target.astype(jnp.float32)[None])
    grad_fields = (weight[None, None] * (own_term - pair / members)).astype(jnp.bfloat16)

    def accumulate(carry, item):
        member_latent, member_grad = item
        pre, hidden, unused = decode(member_latent, w_in, w_out)
        back = lax.dot_general(member_grad, w_out, (((0,), (1,)), ((), ())), preferred_element_type=jnp.float32)
        grad_pre = (back * silu_slope(pre)).astype(jnp.bfloat16)
        grad_in = lax.dot_general(member_latent, grad_pre, (((0,), (0,)), ((), ())), preferred_element_type=jnp.float32)
        grad_out = lax.dot_general(hidden, member_grad, (((0,), (1,)), ((), ())), preferred_element_type=jnp.float32)
        return ((carry[0] + grad_in, carry[1] + grad_out), None)
    start = (jnp.zeros(w_in.shape, jnp.float32), jnp.zeros(w_out.shape, jnp.float32))
    totals, unused = lax.scan(accumulate, start, (latent, grad_fields))
    return (totals[0], totals[1])
```

```python
import functools

import jax
import jax.numpy as jnp
from jax import lax
from jax.experimental import pallas as pl
from jax.experimental.pallas import tpu as pltpu
from jax.sharding import PartitionSpec as P

MESH = pl.DeviceIdType.MESH
BF = jnp.bfloat16
F32 = jnp.float32


def sigmoid(v):
    return 0.5 * jnp.tanh(0.5 * v) + 0.5


def smooth(d):
    return d * lax.rsqrt(1.0 + d * d)


def mm(a, b):
    return jnp.dot(a, b, preferred_element_type=F32)


def body(
    M, CN,
    lat, w_in, w_out, target, mask, out_in, out_out,
    pre, hid, gp, lat_t, hid_t, tgt_t, wgt_t,
    fsend, frecv, gsend, gf,
    acc_f, acc_b, r1, k2, s2, r2, s3, r3, k3,
    sem_fs, sem_fr, sem_gs, sem_gr, sem1s, sem1r, sem2s, sem2r, sem3s, sem3r,
):
    me = lax.axis_index("member")
    cell = lax.axis_index("cell")
    core = lax.rem(cell, 2)
    grp = cell // 2
    G = CN // 2
    N, D = lat.shape
    H = w_in.shape[1]
    FD = w_out.shape[1]
    C = N // M
    PB = M // 2
    r = D // (M * CN)
    scale = 1.0 / (float(N * CN) ** 0.5) / M

    barrier = pltpu.get_barrier_semaphore()
    for d in range(1, M):
        pl.semaphore_signal(barrier, inc=1, device_id=(lax.rem(me + d, M), cell), device_id_type=MESH)
    pl.semaphore_signal(barrier, inc=1, device_id=(me, grp * 2 + 1 - core), device_id_type=MESH)
    for d in range(1, G):
        pl.semaphore_signal(
            barrier, inc=1, device_id=(me, lax.rem(grp + d, G) * 2 + core), device_id_type=MESH
        )
    pl.semaphore_wait(barrier, M - 1 + 1 + G - 1)

    def peer(d):
        return lax.rem(me + d, M)

    def f_copy(d):
        return pltpu.make_async_remote_copy(
            fsend.at[peer(d)], frecv.at[d - 1], sem_fs.at[d - 1], sem_fr.at[d - 1],
            device_id=(peer(d), cell), device_id_type=MESH,
        )

    def g_copy(d):
        return pltpu.make_async_remote_copy(
            gsend.at[d - 1], gf.at[me], sem_gs.at[d - 1], sem_gr.at[d - 1],
            device_id=(lax.rem(me - d + M, M), cell), device_id_type=MESH,
        )

    def c1(i):
        return pltpu.make_async_remote_copy(
            acc_b.at[i, 1 - core], r1.at[i], sem1s.at[i], sem1r.at[i],
            device_id=(me, grp * 2 + 1 - core), device_id_type=MESH,
        )

    def c2(i, d):
        g = lax.rem(grp + d, G)
        return pltpu.make_async_remote_copy(
            s2.at[i, g], r2.at[i, d - 1], sem2s.at[i, d - 1], sem2r.at[i, d - 1],
            device_id=(me, g * 2 + core), device_id_type=MESH,
        )

    def c3(t):
        d = lax.rem(t - me + M, M)
        return pltpu.make_async_remote_copy(
            s3.at[t], r3.at[d - 1], sem3s.at[d - 1], sem3r.at[d - 1],
            device_id=(t, cell), device_id_type=MESH,
        )

    def block_of(i):
        return lax.rem(me // 2 + 1 + i, PB)

    def forward(i, carry):
        p = block_of(i)
        rows = pl.ds(pl.multiple_of(p * (2 * C), 2 * C), 2 * C)
        v = mm(lat[rows, :], w_in[...])
        pre[rows, :] = v
        h = (v * sigmoid(v)).astype(BF)
        hid[rows, :] = h
        f = mm(h, w_out[...]).astype(BF)
        fsend[2 * p] = f[:C]
        fsend[2 * p + 1] = f[C:]
        for s in range(2):
            t = 2 * p + s

            @pl.when(t != me)
            def _():
                f_copy(lax.rem(t - me + M, M)).start()

        return carry

    lax.fori_loop(0, PB, forward, 0)

    wrow = mask[...].astype(F32) * scale
    for b in range(N // 128):
        cols = slice(128 * b, 128 * b + 128)
        tgt_t[cols, :] = target[:, cols].astype(F32).T
        wgt_t[cols, :] = jnp.broadcast_to(wrow[:, cols], (8, 128)).T

    for b in range(N // 128):
        cols = slice(128 * b, 128 * b + 128)
        lat_t[:, cols] = lat[cols, :].T

    for d in range(1, M):
        f_copy(d).wait_recv()

    RB = 16

    def pairs(b, carry):
        rows = pl.ds(pl.multiple_of(b * RB, RB), RB)
        own = pl.ds(pl.multiple_of(me * C + b * RB, RB), RB)
        vals = [frecv[j, rows, :].astype(F32) for j in range(M - 1)]
        vals.append(fsend[me, rows, :].astype(F32))
        t = tgt_t[own, :]
        w = wgt_t[own, 0:1]
        total = [None] * M
        for a in range(M):
            for c in range(a + 1, M):
                k = smooth(vals[a] - vals[c])
                total[a] = k if total[a] is None else total[a] + k
                total[c] = -k if total[c] is None else total[c] - k
        for a in range(M):
            g = (w * (smooth(vals[a] - t) - total[a] * (1.0 / M))).astype(BF)
            if a < M - 1:
                gsend[a, rows, :] = g
            else:
                gf[me, rows, :] = g
        return carry

    lax.fori_loop(0, C // RB, pairs, 0)

    for d in range(1, M):
        g_copy(d).start()

    for b in range(N // 128):
        cols = slice(128 * b, 128 * b + 128)
        hid_t[:, cols] = hid[cols, :].T

    def back(j):
        rows = pl.ds(pl.multiple_of(j * C, C), C)
        q = lax.dot_general(gf[j], w_out[...], (((1,), (1,)), ((), ())), preferred_element_type=F32)
        v = pre[rows, :]
        s = sigmoid(v)
        gp[rows, :] = (q * (s * (1.0 + v * (1.0 - s)))).astype(BF)

    back(me)

    def backs(d, carry):
        pltpu.make_async_remote_copy(
            gsend.at[d - 1], gf.at[lax.rem(me + d, M)], sem_gs.at[d - 1], sem_gr.at[d - 1],
            device_id=(peer(d), cell), device_id_type=MESH,
        ).wait_recv()
        back(lax.rem(me + d, M))
        return carry

    lax.fori_loop(1, M, backs, 0)

    def step(i, carry):
        @pl.when(i < PB)
        def _():
            p = block_of(i)
            rows = pl.ds(pl.multiple_of(p * (2 * r * CN), 2 * r * CN), 2 * r * CN)
            a = mm(lat_t[rows, :], gp[...])
            b = mm(hid_t[rows, :], gf[...].reshape(N, FD))
            for s in range(2):
                for c in range(CN):
                    at = (s * CN + c) * r
                    x, y = a[at : at + r], b[at : at + r]
                    acc_f[i, c % 2, s, c // 2, :, :H] = x
                    acc_f[i, c % 2, s, c // 2, :, H : H + FD] = y
                    acc_b[i, c % 2, s, c // 2, :, :H] = x.astype(BF)
                    acc_b[i, c % 2, s, c // 2, :, H : H + FD] = y.astype(BF)
            c1(i).start()

        @pl.when((i >= 1) & (i <= PB))
        def _():
            j = i - 1
            c1(j).wait_recv()
            for g in range(G):
                for s in range(2):
                    v = acc_f[j, core, s, g] + r1[j, s, g].astype(F32)
                    k2[j, g, s] = v
                    s2[j, g, s] = v.astype(BF)
            for d in range(1, G):
                c2(j, d).start()

        @pl.when(i >= 2)
        def _():
            j = i - 2
            p = block_of(j)
            for d in range(1, G):
                c2(j, d).wait_recv()
            for s in range(2):
                v = k2[j, grp, s]
                for d in range(1, G):
                    v = v + r2[j, d - 1, s].astype(F32)
                t = 2 * p + s
                s3[t] = v.astype(BF)

                @pl.when(t == me)
                def _():
                    k3[...] = v

                @pl.when(t != me)
                def _():
                    c3(t).start()

        return carry

    lax.fori_loop(0, PB + 2, step, 0)

    total = k3[...]
    for d in range(1, M):
        pltpu.make_async_remote_copy(
            s3.at[0], r3.at[d - 1], sem3s.at[d - 1], sem3r.at[d - 1],
            device_id=(peer(d), cell), device_id_type=MESH,
        ).wait_recv()
        total = total + r3[d - 1].astype(F32)
    out_in[...] = total[:, :H]
    out_out[...] = total[:, H : H + FD]

    for d in range(1, M):
        f_copy(d).wait_send()
        g_copy(d).wait_send()
        c3(peer(d)).wait_send()
    for i in range(PB):
        c1(i).wait_send()
        for d in range(1, G):
            c2(i, d).wait_send()


def per_device(latent, w_in, w_out, target, cell_mask):
    M = lax.axis_size("member")
    CN = lax.axis_size("cell")
    N, D = latent.shape[1:]
    H = w_in.shape[1]
    FD = w_out.shape[1]
    C, PB, G = N // M, M // 2, CN // 2
    r = D // (M * CN)
    W = H + (FD + 127) // 128 * 128
    V = pltpu.VMEM
    DMA = pltpu.SemaphoreType.DMA
    GS = max(G - 1, 1)
    vm = pl.BlockSpec(memory_space=pltpu.VMEM)
    return pl.pallas_call(
        functools.partial(body, M, CN),
        out_shape=(
            jax.ShapeDtypeStruct((r, H), F32),
            jax.ShapeDtypeStruct((r, FD), F32),
        ),
        in_specs=[vm] * 5,
        out_specs=(vm, vm),
        scratch_shapes=[
            V((N, H), F32), V((N, H), BF), V((N, H), BF), V((D, N), BF), V((H, N), BF),
            V((N, FD), F32), V((N, 8), F32),
            V((M, C, FD), BF), V((M - 1, C, FD), BF), V((M - 1, C, FD), BF), V((M, C, FD), BF),
            V((PB, 2, 2, G, r, W), F32), V((PB, 2, 2, G, r, W), BF), V((PB, 2, G, r, W), BF),
            V((PB, G, 2, r, W), F32), V((PB, G, 2, r, W), BF), V((PB, GS, 2, r, W), BF),
            V((M, r, W), BF), V((M - 1, r, W), BF), V((r, W), F32),
            DMA((M - 1,)), DMA((M - 1,)), DMA((M - 1,)), DMA((M - 1,)),
            DMA((PB,)), DMA((PB,)), DMA((PB, GS)), DMA((PB, GS)),
            DMA((M - 1,)), DMA((M - 1,)),
        ],
        compiler_params=pltpu.CompilerParams(
            collective_id=0, has_side_effects=True, vmem_limit_bytes=60 * 1024 * 1024
        ),
    )(latent[0], w_in, w_out, target, cell_mask.reshape(1, N))


def solution(mesh):
    in_specs = (P("member", "cell", None), P(), P(), P(None, "cell"), P("cell"))
    out_specs = (P(("member", "cell"), None), P(("member", "cell"), None))
    return jax.shard_map(
        per_device, mesh=mesh, in_specs=in_specs, out_specs=out_specs, check_vma=False
    )
```

```python
import functools

import jax
import jax.numpy as jnp
from jax import lax
from jax.experimental import pallas as pl
from jax.experimental.pallas import tpu as pltpu
from jax.sharding import PartitionSpec as P

MESH = pl.DeviceIdType.MESH
BF = jnp.bfloat16
F32 = jnp.float32


def sigmoid(v):
    return 0.5 * jnp.tanh(0.5 * v) + 0.5


def smooth(d):
    return d * lax.rsqrt(1.0 + d * d)


def mm(a, b):
    return jnp.dot(a, b, preferred_element_type=F32)


def body(
    M, CN,
    lat_hbm, w_in_hbm, w_out, target, mask, out_in, out_out,
    lat, w_in, slope, hid, gp, sums, tgt_t, wgt_t,
    fsend, frecv, gsend, gf,
    acc_f, acc_b, r1, k2, s2, r2, s3, r3, k3,
    sem_in, sem_fs, sem_fr, sem_gs, sem_gr, sem1s, sem1r, sem2s, sem2r, sem3s, sem3r,
):
    me = lax.axis_index("member")
    cell = lax.axis_index("cell")
    core = lax.rem(cell, 2)
    grp = cell // 2
    G = CN // 2
    N, D = lat.shape
    H = w_in.shape[1]
    FD = w_out.shape[0]
    C = N // M
    PB = M // 2
    r = D // (M * CN)
    scale = 1.0 / (float(N * CN) ** 0.5) / M

    def block_of(i):
        return lax.rem(me // 2 + 1 + i, PB)

    def load(i):
        rows = pl.ds(pl.multiple_of(block_of(i) * (2 * C), 2 * C), 2 * C)
        return pltpu.make_async_copy(lat_hbm.at[rows, :], lat.at[rows, :], sem_in.at[i])

    load_w = pltpu.make_async_copy(w_in_hbm, w_in, sem_in.at[PB])
    load_w.start()
    for i in range(PB):
        load(i).start()

    barrier = pltpu.get_barrier_semaphore()
    for d in range(1, M):
        pl.semaphore_signal(barrier, inc=1, device_id=(lax.rem(me + d, M), cell), device_id_type=MESH)
    pl.semaphore_signal(barrier, inc=1, device_id=(me, grp * 2 + 1 - core), device_id_type=MESH)
    for d in range(1, G):
        pl.semaphore_signal(
            barrier, inc=1, device_id=(me, lax.rem(grp + d, G) * 2 + core), device_id_type=MESH
        )

    for b in range(N // 128):
        cols = slice(128 * b, 128 * b + 128)
        tgt_t[cols, :] = target[:, cols].astype(F32).T
        w = mask[cols].astype(F32) * scale
        wgt_t[cols, :] = jnp.broadcast_to(w[None, :], (8, 128)).T

    pl.semaphore_wait(barrier, M - 1 + 1 + G - 1)

    def peer(d):
        return lax.rem(me + d, M)

    def f_copy(d):
        return pltpu.make_async_remote_copy(
            fsend.at[peer(d)], frecv.at[d - 1], sem_fs.at[d - 1], sem_fr.at[d - 1],
            device_id=(peer(d), cell), device_id_type=MESH,
        )

    def g_copy(d):
        return pltpu.make_async_remote_copy(
            gsend.at[d - 1], gf.at[me], sem_gs.at[d - 1], sem_gr.at[d - 1],
            device_id=(lax.rem(me - d + M, M), cell), device_id_type=MESH,
        )

    def c1(i):
        return pltpu.make_async_remote_copy(
            acc_b.at[i, 1 - core], r1.at[i], sem1s.at[i], sem1r.at[i],
            device_id=(me, grp * 2 + 1 - core), device_id_type=MESH,
        )

    def c2(i, d):
        g = lax.rem(grp + d, G)
        return pltpu.make_async_remote_copy(
            s2.at[i, g], r2.at[i, d - 1], sem2s.at[i, d - 1], sem2r.at[i, d - 1],
            device_id=(me, g * 2 + core), device_id_type=MESH,
        )

    def c3(t):
        d = lax.rem(t - me + M, M)
        return pltpu.make_async_remote_copy(
            s3.at[t], r3.at[d - 1], sem3s.at[d - 1], sem3r.at[d - 1],
            device_id=(t, cell), device_id_type=MESH,
        )

    def forward(i, carry):
        p = block_of(i)
        rows = pl.ds(pl.multiple_of(p * (2 * C), 2 * C), 2 * C)
        load(i).wait()
        v = mm(lat[rows, :], w_in[...])
        s = sigmoid(v)
        slope[rows, :] = s * (1.0 + v * (1.0 - s))
        h = (v * s).astype(BF)
        hid[rows, :] = h
        f = lax.dot_general(
            h, w_out[...], (((1,), (1,)), ((), ())), preferred_element_type=F32
        ).astype(BF)
        fsend[2 * p] = f[:C]
        fsend[2 * p + 1] = f[C:]
        for s in range(2):
            t = 2 * p + s

            @pl.when(t != me)
            def _():
                f_copy(lax.rem(t - me + M, M)).start()

        return carry

    load_w.wait()
    lax.fori_loop(0, PB, forward, 0)

    sums[...] = jnp.zeros_like(sums)
    for d in range(1, M):
        f_copy(d).wait_recv()

    RB = 16

    def pairs(b, carry):
        rows = pl.ds(pl.multiple_of(b * RB, RB), RB)
        own = pl.ds(pl.multiple_of(me * C + b * RB, RB), RB)
        vals = [frecv[j, rows, :].astype(F32) for j in range(M - 1)]
        vals.append(fsend[me, rows, :].astype(F32))
        t = tgt_t[own, :]
        w = wgt_t[own, 0:1]
        total = [None] * M
        for a in range(M):
            for c in range(a + 1, M):
                k = smooth(vals[a] - vals[c])
                total[a] = k if total[a] is None else total[a] + k
                total[c] = -k if total[c] is None else total[c] - k
        for a in range(M):
            g = (w * (smooth(vals[a] - t) - total[a] * (1.0 / M))).astype(BF)
            if a < M - 1:
                gsend[a, rows, :] = g
            else:
                gf[me, rows, :] = g
        return carry

    lax.fori_loop(0, C // RB, pairs, 0)

    g_copy(lax.rem(me - (me + 1 - 2 * lax.rem(me, 2)) + M, M)).start()
    for i in range(1, PB):
        p = lax.rem(me // 2 - i + PB, PB)
        for e in range(2):
            g_copy(lax.rem(me - (2 * p + e) + M, M)).start()

    T = 2 * r * CN

    def tile(p, q):
        rows = pl.ds(pl.multiple_of(p * (2 * C), 2 * C), 2 * C)
        cols = pl.ds(pl.multiple_of(q * T, T), T)
        over = (((0,), (0,)), ((), ()))
        g = gf[pl.ds(2 * p, 2)].reshape(2 * C, FD)
        a = lax.dot_general(lat[rows, cols], gp[rows, :], over, preferred_element_type=F32)
        b = lax.dot_general(hid[rows, cols], g, over, preferred_element_type=F32)
        to = pl.ds(pl.multiple_of(q * T, T), T)
        return a + sums[to, :H], b + sums[to, H : H + FD]

    def backs(k, carry):
        p = lax.rem(me // 2 + k, PB)
        for e in range(2):
            j = 2 * p + e

            @pl.when(j != me)
            def _():
                d = lax.rem(j - me + M, M)
                pltpu.make_async_remote_copy(
                    gsend.at[d - 1], gf.at[j], sem_gs.at[d - 1], sem_gr.at[d - 1],
                    device_id=(j, cell), device_id_type=MESH,
                ).wait_recv()

        rows = pl.ds(pl.multiple_of(p * (2 * C), 2 * C), 2 * C)
        g = gf[pl.ds(2 * p, 2)].reshape(2 * C, FD)
        gp[rows, :] = (mm(g, w_out[...]) * slope[rows, :]).astype(BF)

        @pl.when(k < PB - 1)
        def _():
            def more(q, c):
                a, b = tile(p, q)
                to = pl.ds(pl.multiple_of(q * T, T), T)
                sums[to, :H] = a
                sums[to, H : H + FD] = b
                return c

            lax.fori_loop(0, PB, more, 0)

        return carry

    lax.fori_loop(0, PB, backs, 0)

    def step(i, carry):
        @pl.when(i < PB)
        def _():
            p = block_of(i)
            a, b = tile(lax.rem(me // 2 + PB - 1, PB), p)
            for s in range(2):
                for c in range(CN):
                    at = (s * CN + c) * r
                    x, y = a[at : at + r], b[at : at + r]
                    acc_f[i, c % 2, s, c // 2, :, :H] = x
                    acc_f[i, c % 2, s, c // 2, :, H : H + FD] = y
                    acc_b[i, c % 2, s, c // 2, :, :H] = x.astype(BF)
                    acc_b[i, c % 2, s, c // 2, :, H : H + FD] = y.astype(BF)
            c1(i).start()

        @pl.when((i >= 1) & (i <= PB))
        def _():
            j = i - 1
            c1(j).wait_recv()
            for g in range(G):
                for s in range(2):
                    v = acc_f[j, core, s, g] + r1[j, s, g].astype(F32)
                    k2[j, g, s] = v
                    s2[j, g, s] = v.astype(BF)
            for d in range(1, G):
                c2(j, d).start()

        @pl.when(i >= 2)
        def _():
            j = i - 2
            p = block_of(j)
            for d in range(1, G):
                c2(j, d).wait_recv()
            for s in range(2):
                v = k2[j, grp, s]
                for d in range(1, G):
                    v = v + r2[j, d - 1, s].astype(F32)
                t = 2 * p + s
                s3[t] = v.astype(BF)

                @pl.when(t == me)
                def _():
                    k3[...] = v

                @pl.when(t != me)
                def _():
                    c3(t).start()

        return carry

    lax.fori_loop(0, PB + 2, step, 0)

    total = k3[...]
    for d in range(1, M):
        pltpu.make_async_remote_copy(
            s3.at[0], r3.at[d - 1], sem3s.at[d - 1], sem3r.at[d - 1],
            device_id=(peer(d), cell), device_id_type=MESH,
        ).wait_recv()
        total = total + r3[d - 1].astype(F32)
    out_in[...] = total[:, :H]
    out_out[...] = total[:, H : H + FD]

    for d in range(1, M):
        f_copy(d).wait_send()
        g_copy(d).wait_send()
        c3(peer(d)).wait_send()
    for i in range(PB):
        c1(i).wait_send()
        for d in range(1, G):
            c2(i, d).wait_send()


def per_device(latent, w_in, w_out, target, cell_mask):
    M = lax.axis_size("member")
    CN = lax.axis_size("cell")
    N, D = latent.shape[1:]
    H = w_in.shape[1]
    FD = w_out.shape[1]
    C, PB, G = N // M, M // 2, CN // 2
    r = D // (M * CN)
    W = H + (FD + 127) // 128 * 128
    V = pltpu.VMEM
    DMA = pltpu.SemaphoreType.DMA
    GS = max(G - 1, 1)
    vm = pl.BlockSpec(memory_space=pltpu.VMEM)
    return pl.pallas_call(
        functools.partial(body, M, CN),
        out_shape=(
            jax.ShapeDtypeStruct((r, H), F32),
            jax.ShapeDtypeStruct((r, FD), F32),
        ),
        in_specs=[pl.BlockSpec(memory_space=pl.ANY)] * 2 + [vm] * 3,
        out_specs=(vm, vm),
        scratch_shapes=[
            V((N, D), BF), V((D, H), BF), V((N, H), F32), V((N, H), BF), V((N, H), BF), V((D, W), F32),
            V((N, FD), F32), V((N, 8), F32),
            V((M, C, FD), BF), V((M - 1, C, FD), BF), V((M - 1, C, FD), BF), V((M, C, FD), BF),
            V((PB, 2, 2, G, r, W), F32), V((PB, 2, 2, G, r, W), BF), V((PB, 2, G, r, W), BF),
            V((PB, G, 2, r, W), F32), V((PB, G, 2, r, W), BF), V((PB, GS, 2, r, W), BF),
            V((M, r, W), BF), V((M - 1, r, W), BF), V((r, W), F32),
            DMA((PB + 1,)), DMA((M - 1,)), DMA((M - 1,)), DMA((M - 1,)), DMA((M - 1,)),
            DMA((PB,)), DMA((PB,)), DMA((PB, GS)), DMA((PB, GS)),
            DMA((M - 1,)), DMA((M - 1,)),
        ],
        compiler_params=pltpu.CompilerParams(
            collective_id=0, has_side_effects=True, vmem_limit_bytes=60 * 1024 * 1024
        ),
    )(latent[0], w_in, w_out.T, target, cell_mask)


def solution(mesh):
    in_specs = (P("member", "cell", None), P(), P(), P(None, "cell"), P("cell"))
    out_specs = (P(("member", "cell"), None), P(("member", "cell"), None))
    return jax.shard_map(
        per_device, mesh=mesh, in_specs=in_specs, out_specs=out_specs, check_vma=False
    )
```

```python
import functools

import jax
import jax.numpy as jnp
from jax import lax
from jax.experimental import pallas as pl
from jax.experimental.pallas import tpu as pltpu
from jax.sharding import PartitionSpec as P

MESH = pl.DeviceIdType.MESH
BF = jnp.bfloat16
F32 = jnp.float32


def sigmoid(v):
    return 0.5 * jnp.tanh(0.5 * v) + 0.5


def smooth(d):
    return d * lax.rsqrt(1.0 + d * d)


def mm(a, b):
    return jnp.dot(a, b, preferred_element_type=F32)


def body(
    M, CN,
    lat_hbm, w_in_hbm, w_out, target, mask, out_in, out_out,
    lat, w_in, slope, hid, gp, lat_t, hid_t, tgt_t, wgt_t,
    fsend, frecv, gsend, gf,
    acc_f, acc_b, r1, k2, s2, r2, s3, r3, k3,
    sem_in, sem_fs, sem_fr, sem_gs, sem_gr, sem1s, sem1r, sem2s, sem2r, sem3s, sem3r,
):
    me = lax.axis_index("member")
    cell = lax.axis_index("cell")
    core = lax.rem(cell, 2)
    grp = cell // 2
    G = CN // 2
    N, D = lat.shape
    H = w_in.shape[1]
    FD = w_out.shape[0]
    C = N // M
    PB = M // 2
    r = D // (M * CN)
    scale = 1.0 / (float(N * CN) ** 0.5) / M

    def block_of(i):
        return lax.rem(me // 2 + 1 + i, PB)

    def load(i):
        rows = pl.ds(pl.multiple_of(block_of(i) * (2 * C), 2 * C), 2 * C)
        return pltpu.make_async_copy(lat_hbm.at[rows, :], lat.at[rows, :], sem_in.at[i])

    load_w = pltpu.make_async_copy(w_in_hbm, w_in, sem_in.at[PB])
    load_w.start()
    for i in range(PB):
        load(i).start()

    barrier = pltpu.get_barrier_semaphore()
    for d in range(1, M):
        pl.semaphore_signal(barrier, inc=1, device_id=(lax.rem(me + d, M), cell), device_id_type=MESH)
    pl.semaphore_signal(barrier, inc=1, device_id=(me, grp * 2 + 1 - core), device_id_type=MESH)
    for d in range(1, G):
        pl.semaphore_signal(
            barrier, inc=1, device_id=(me, lax.rem(grp + d, G) * 2 + core), device_id_type=MESH
        )

    for b in range(N // 128):
        cols = slice(128 * b, 128 * b + 128)
        tgt_t[cols, :] = target[:, cols].astype(F32).T
        w = mask[cols].astype(F32) * scale
        wgt_t[cols, :] = jnp.broadcast_to(w[None, :], (8, 128)).T

    pl.semaphore_wait(barrier, M - 1 + 1 + G - 1)

    def peer(d):
        return lax.rem(me + d, M)

    def f_copy(d):
        return pltpu.make_async_remote_copy(
            fsend.at[peer(d)], frecv.at[d - 1], sem_fs.at[d - 1], sem_fr.at[d - 1],
            device_id=(peer(d), cell), device_id_type=MESH,
        )

    def g_copy(d):
        return pltpu.make_async_remote_copy(
            gsend.at[d - 1], gf.at[me], sem_gs.at[d - 1], sem_gr.at[d - 1],
            device_id=(lax.rem(me - d + M, M), cell), device_id_type=MESH,
        )

    def c1(i):
        return pltpu.make_async_remote_copy(
            acc_b.at[i, 1 - core], r1.at[i], sem1s.at[i], sem1r.at[i],
            device_id=(me, grp * 2 + 1 - core), device_id_type=MESH,
        )

    def c2(i, d):
        g = lax.rem(grp + d, G)
        return pltpu.make_async_remote_copy(
            s2.at[i, g], r2.at[i, d - 1], sem2s.at[i, d - 1], sem2r.at[i, d - 1],
            device_id=(me, g * 2 + core), device_id_type=MESH,
        )

    def c3(t):
        d = lax.rem(t - me + M, M)
        return pltpu.make_async_remote_copy(
            s3.at[t], r3.at[d - 1], sem3s.at[d - 1], sem3r.at[d - 1],
            device_id=(t, cell), device_id_type=MESH,
        )

    def forward(i, carry):
        p = block_of(i)
        rows = pl.ds(pl.multiple_of(p * (2 * C), 2 * C), 2 * C)
        load(i).wait()
        v = mm(lat[rows, :], w_in[...])
        s = sigmoid(v)
        slope[rows, :] = s * (1.0 + v * (1.0 - s))
        h = (v * s).astype(BF)
        hid[rows, :] = h
        f = lax.dot_general(
            h, w_out[...], (((1,), (1,)), ((), ())), preferred_element_type=F32
        ).astype(BF)
        fsend[2 * p] = f[:C]
        fsend[2 * p + 1] = f[C:]
        for s in range(2):
            t = 2 * p + s

            @pl.when(t != me)
            def _():
                f_copy(lax.rem(t - me + M, M)).start()

        return carry

    load_w.wait()
    lax.fori_loop(0, PB, forward, 0)

    for b in range(N // 128):
        cols = slice(128 * b, 128 * b + 128)
        lat_t[:, cols] = lat[cols, :].T

    for d in range(1, M):
        f_copy(d).wait_recv()

    RB = 16

    def pairs(b, carry):
        rows = pl.ds(pl.multiple_of(b * RB, RB), RB)
        own = pl.ds(pl.multiple_of(me * C + b * RB, RB), RB)
        vals = [frecv[j, rows, :].astype(F32) for j in range(M - 1)]
        vals.append(fsend[me, rows, :].astype(F32))
        t = tgt_t[own, :]
        w = wgt_t[own, 0:1]
        total = [None] * M
        for a in range(M):
            for c in range(a + 1, M):
                k = smooth(vals[a] - vals[c])
                total[a] = k if total[a] is None else total[a] + k
                total[c] = -k if total[c] is None else total[c] - k
        for a in range(M):
            g = (w * (smooth(vals[a] - t) - total[a] * (1.0 / M))).astype(BF)
            if a < M - 1:
                gsend[a, rows, :] = g
            else:
                gf[me, rows, :] = g
        return carry

    lax.fori_loop(0, C // RB, pairs, 0)

    for d in range(1, M):
        g_copy(d).start()

    for b in range(N // 128):
        cols = slice(128 * b, 128 * b + 128)
        hid_t[:, cols] = hid[cols, :].T

    def back(j):
        rows = pl.ds(pl.multiple_of(j * C, C), C)
        gp[rows, :] = (mm(gf[j], w_out[...]) * slope[rows, :]).astype(BF)

    back(me)

    def backs(d, carry):
        pltpu.make_async_remote_copy(
            gsend.at[d - 1], gf.at[lax.rem(me + d, M)], sem_gs.at[d - 1], sem_gr.at[d - 1],
            device_id=(peer(d), cell), device_id_type=MESH,
        ).wait_recv()
        back(lax.rem(me + d, M))
        return carry

    lax.fori_loop(1, M, backs, 0)

    def step(i, carry):
        @pl.when(i < PB)
        def _():
            p = block_of(i)
            rows = pl.ds(pl.multiple_of(p * (2 * r * CN), 2 * r * CN), 2 * r * CN)
            a = mm(lat_t[rows, :], gp[...])
            b = mm(hid_t[rows, :], gf[...].reshape(N, FD))
            for s in range(2):
                for c in range(CN):
                    at = (s * CN + c) * r
                    x, y = a[at : at + r], b[at : at + r]
                    acc_f[i, c % 2, s, c // 2, :, :H] = x
                    acc_f[i, c % 2, s, c // 2, :, H : H + FD] = y
                    acc_b[i, c % 2, s, c // 2, :, :H] = x.astype(BF)
                    acc_b[i, c % 2, s, c // 2, :, H : H + FD] = y.astype(BF)
            c1(i).start()

        @pl.when((i >= 1) & (i <= PB))
        def _():
            j = i - 1
            c1(j).wait_recv()
            for g in range(G):
                for s in range(2):
                    v = acc_f[j, core, s, g] + r1[j, s, g].astype(F32)
                    k2[j, g, s] = v
                    s2[j, g, s] = v.astype(BF)
            for d in range(1, G):
                c2(j, d).start()

        @pl.when(i >= 2)
        def _():
            j = i - 2
            p = block_of(j)
            for d in range(1, G):
                c2(j, d).wait_recv()
            for s in range(2):
                v = k2[j, grp, s]
                for d in range(1, G):
                    v = v + r2[j, d - 1, s].astype(F32)
                t = 2 * p + s
                s3[t] = v.astype(BF)

                @pl.when(t == me)
                def _():
                    k3[...] = v

                @pl.when(t != me)
                def _():
                    c3(t).start()

        return carry

    lax.fori_loop(0, PB + 2, step, 0)

    total = k3[...]
    for d in range(1, M):
        pltpu.make_async_remote_copy(
            s3.at[0], r3.at[d - 1], sem3s.at[d - 1], sem3r.at[d - 1],
            device_id=(peer(d), cell), device_id_type=MESH,
        ).wait_recv()
        total = total + r3[d - 1].astype(F32)
    out_in[...] = total[:, :H]
    out_out[...] = total[:, H : H + FD]

    for d in range(1, M):
        f_copy(d).wait_send()
        g_copy(d).wait_send()
        c3(peer(d)).wait_send()
    for i in range(PB):
        c1(i).wait_send()
        for d in range(1, G):
            c2(i, d).wait_send()


def per_device(latent, w_in, w_out, target, cell_mask):
    M = lax.axis_size("member")
    CN = lax.axis_size("cell")
    N, D = latent.shape[1:]
    H = w_in.shape[1]
    FD = w_out.shape[1]
    C, PB, G = N // M, M // 2, CN // 2
    r = D // (M * CN)
    W = H + (FD + 127) // 128 * 128
    V = pltpu.VMEM
    DMA = pltpu.SemaphoreType.DMA
    GS = max(G - 1, 1)
    vm = pl.BlockSpec(memory_space=pltpu.VMEM)
    return pl.pallas_call(
        functools.partial(body, M, CN),
        out_shape=(
            jax.ShapeDtypeStruct((r, H), F32),
            jax.ShapeDtypeStruct((r, FD), F32),
        ),
        in_specs=[pl.BlockSpec(memory_space=pl.ANY)] * 2 + [vm] * 3,
        out_specs=(vm, vm),
        scratch_shapes=[
            V((N, D), BF), V((D, H), BF), V((N, H), F32), V((N, H), BF), V((N, H), BF), V((D, N), BF), V((H, N), BF),
            V((N, FD), F32), V((N, 8), F32),
            V((M, C, FD), BF), V((M - 1, C, FD), BF), V((M - 1, C, FD), BF), V((M, C, FD), BF),
            V((PB, 2, 2, G, r, W), F32), V((PB, 2, 2, G, r, W), BF), V((PB, 2, G, r, W), BF),
            V((PB, G, 2, r, W), F32), V((PB, G, 2, r, W), BF), V((PB, GS, 2, r, W), BF),
            V((M, r, W), BF), V((M - 1, r, W), BF), V((r, W), F32),
            DMA((PB + 1,)), DMA((M - 1,)), DMA((M - 1,)), DMA((M - 1,)), DMA((M - 1,)),
            DMA((PB,)), DMA((PB,)), DMA((PB, GS)), DMA((PB, GS)),
            DMA((M - 1,)), DMA((M - 1,)),
        ],
        compiler_params=pltpu.CompilerParams(
            collective_id=0, has_side_effects=True, vmem_limit_bytes=60 * 1024 * 1024
        ),
    )(latent[0], w_in, w_out.T, target, cell_mask)


def solution(mesh):
    in_specs = (P("member", "cell", None), P(), P(), P(None, "cell"), P("cell"))
    out_specs = (P(("member", "cell"), None), P(("member", "cell"), None))
    return jax.shard_map(
        per_device, mesh=mesh, in_specs=in_specs, out_specs=out_specs, check_vma=False
    )
```
